256 devices in a mesh: rep: 8 (over z_lo, y), inner: 32 (over z_hi, x, core).
Axes of the slice: x: 4, y: 4, z: 8 (z_hi: 4, z_lo: 2; z = z_hi * 2 + z_lo), core: 2. Of those that a mesh axis runs over, the one named last changes fastest.
Arguments:
- local_weights: float32 [8, 12, 1600, 1600], P('rep', None, 'inner'), may hold values from -6 to 6
- owner_global: float32 [32, 1600, 1600], P('inner', None, 'rep'), may hold values from -6 to 6
- owner_momentum: float32 [32, 1600, 1600], P('inner', None, 'rep'), may hold values from -6 to 6
- owner_list: int32 [12], replicated, may hold values from 0 to 31, as said below
- local_down: float32 [8, 6400, 1600], P('rep', 'inner'), may hold values from -6 to 6
- global_down: float32 [6400, 1600], P('inner', 'rep'), may hold values from -6 to 6
- down_basis: float32 [6400, 64], P('inner'), may hold values from -0.15625 to 0.15625
- coef_momentum: float32 [64, 1600], P(None, 'rep'), may hold values from -6 to 6
Outputs:
- new_weights: float32 [12, 1600, 1600], P(None, 'inner')
- momentum_out: float32 [32, 1600, 1600], P('inner', None, 'rep')
- new_down: float32 [6400, 1600], P('inner', 'rep')
- coef_new: float32 [64, 1600], P(None, 'rep')
The draws below stay inside these ranges and needn't reach their ends.
Inputs may be any that keep to these rules, and one draw needn't show every extreme that they name: `owner_list`: the 12 entries are distinct inner indices; both ends of the range are owners.
All inputs are finite; a program needn't handle non-finite values.
Results may differ from the reference program's by a relative error of at most 0.00007.
Values sent between devices are 32-bit elements; how exact they have to be, the bound alone decides.
A program may use at most 128 MiB of HBM per device.

```python
import jax
import jax.numpy as jnp
from jax import lax

D = 1600
FF = 6400
RANK = 64
MATS = 12
REPS = 8
OWNERS = 32
N_INNER = 32


def draw_owner_list(key, part):
    first_key = jax.random.fold_in(key, 11)
    second_key = jax.random.fold_in(key, 23)
    middle = 1 + jax.random.permutation(first_key, N_INNER - 2).astype(jnp.int32)
    ends = jnp.array([0, N_INNER - 1], dtype=jnp.int32)
    chosen = jnp.concatenate([ends, middle[:MATS - 2].astype(jnp.int32)])
    order = jax.random.permutation(second_key, MATS).astype(jnp.int32)
    return chosen[order].astype(jnp.int32)


def block_scale(rng, dims, split, low, high):
    loudness, own = 1.0, jax.random.fold_in(rng, 6)
    for position, parts in split:
        steps = jnp.exp(jax.random.uniform(jax.random.fold_in(own, position), (parts,), jnp.float32, low / len(split), high / len(split)))
        loudness = loudness * jnp.repeat(steps, dims[position] // parts).reshape([-1 if axis == position else 1 for axis in range(len(dims))])
    return loudness


def bell_draw(stream_key, shape, spread, most, shards=(), kind=jnp.bfloat16):
    values = jax.random.normal(stream_key, shape, jnp.float32) * spread
    if len(shards) > 0:
        values = block_scale(stream_key, shape, shards, -0.22, 0.18) * values
    return jnp.clip(values, min=-most, max=most).astype(kind)


def setup_inputs(seed: int = 0) -> dict:
    keys = jax.random.split(jax.random.key(seed), 9)
    local_weights = bell_draw(keys[0], (REPS, MATS, D, D), 1.0, 6.0, ((0, 8), (2, 32)), jnp.float32)
    owner_global = bell_draw(keys[1], (OWNERS, D, D), 1.0, 6.0, ((0, 32), (2, 8)), jnp.float32)
    owner_momentum = bell_draw(keys[2], (OWNERS, D, D), 1.0, 6.0, ((0, 32), (2, 8)), jnp.float32)
    owner_list = draw_owner_list(jax.random.fold_in(keys[8], 71), 0)
    local_down = bell_draw(keys[4], (REPS, FF, D), 1.0, 6.0, ((0, 8), (1, 32)), jnp.float32)
    global_down = bell_draw(keys[5], (FF, D), 1.0, 6.0, ((0, 32), (1, 8)), jnp.float32)
    down_basis = bell_draw(keys[6], (FF, RANK), D ** -0.5, 0.15625, ((0, 32),), jnp.float32)
    coef_momentum = bell_draw(keys[7], (RANK, D), 1.0, 6.0, ((1, 8),), jnp.float32)
    return {"local_weights": local_weights, "owner_global": owner_global, "owner_momentum": owner_momentum, "owner_list": owner_list, "local_down": local_down, "global_down": global_down, "down_basis": down_basis, "coef_momentum": coef_momentum}


outer_momentum = 0.9
outer_rate = 0.7


def reference(local_weights, owner_global, owner_momentum, owner_list, local_down, global_down, down_basis, coef_momentum):
    average = jnp.sum(local_weights, axis=0) / REPS
    current = owner_global[owner_list]
    moment = owner_momentum[owner_list]
    delta = current - average
    moment_new = outer_momentum * moment + delta
    new_weights = current - outer_rate * (delta + outer_momentum * moment_new)
    momentum_out = jnp.zeros_like(owner_momentum).at[owner_list].set(moment_new)
    down_diff = global_down - jnp.sum(local_down, axis=0) / REPS
    coef_step = jnp.dot(down_basis.T, down_diff, precision=lax.Precision.HIGHEST, preferred_element_type=jnp.float32)
    coef_new = outer_momentum * coef_momentum + coef_step
    change = jnp.dot(down_basis, coef_step + outer_momentum * coef_new, precision=lax.Precision.HIGHEST, preferred_element_type=jnp.float32)
    new_down = global_down - outer_rate * change
    return new_weights, momentum_out, new_down, coef_new
```

```python
import jax
import jax.numpy as jnp
from jax import lax
from jax.experimental import pallas as pl
from jax.experimental.pallas import tpu as pltpu
from jax.sharding import PartitionSpec as P

MESH = pl.DeviceIdType.MESH
HIGHEST = lax.Precision.HIGHEST
F32 = jnp.float32

outer_momentum = 0.9
outer_rate = 0.7

D = 1600
MATS = 12
HALF = MATS // 2
GROUPS = 8
OWNERS = 32
WIDTH = D // GROUPS
SLAB = D // OWNERS
RANK = 64
FOLD = 5
SUB = WIDTH // FOLD
LANES = 256
Y, ZLO, ZHI, XC = 4, 2, 4, 8

AVERAGE_PART = outer_rate * (1.0 + outer_momentum)
CURRENT_PART = 1.0 - AVERAGE_PART
MOMENT_PART = -outer_rate * outer_momentum * outer_momentum


def fold_lanes(parts):
    pad = jnp.zeros(parts[0].shape[:-1] + (LANES - FOLD * SLAB,), F32)
    return jnp.concatenate(list(parts) + [pad], axis=-1)


def pack_kernel(w_ref, g_ref, m_ref, bt_ref, ld_ref, gd_ref, wp_ref, bp_ref, cp_ref):
    cols = w_ref[0].T.reshape(ZLO, Y, FOLD, SUB, SLAB)
    wp_ref[:, 0] = fold_lanes([cols[:, :, g] for g in range(FOLD)]).transpose(1, 0, 2, 3)

    @pl.when(pl.program_id(0) == 0)
    def _():
        b = (CURRENT_PART * g_ref[...] + MOMENT_PART * m_ref[...]).reshape(FOLD, SUB, D)
        for i in range(OWNERS):
            bp_ref[i] = fold_lanes([b[g][:, SLAB * i : SLAB * (i + 1)] for g in range(FOLD)])

    @pl.when(pl.program_id(0) == 1)
    def _():
        rep = lax.axis_index("rep")
        local = jnp.dot(bt_ref[...], ld_ref[...], precision=HIGHEST, preferred_element_type=F32)
        mine = jnp.dot(bt_ref[...], gd_ref[...], precision=HIGHEST, preferred_element_type=F32)
        pad = jnp.zeros((RANK, LANES - WIDTH), F32)
        for r in range(GROUPS):
            part = local[:, WIDTH * r : WIDTH * (r + 1)] * (-1.0 / GROUPS)
            part = part + jnp.where(rep == r, mine, 0.0)
            cp_ref[:, r % Y, r // Y] = jnp.concatenate([part, pad], axis=-1).reshape(
                XC, RANK // XC, LANES
            )


def comm_kernel(
    list_ref, wp, bp, cp, out, arec, coef,
    r1p, r1m, r2p, r2m, sp, sm, rz, ssum, avg, brec, asend,
    d1, d2, d3, d4, e2, f2, g2,
    s_one, s_two, s_rel, s_z, s_own, s_fwd, s_far, s_b, s_a, s_d1, s_d2, s_dz, s_d3, s_d4,
    q_one, q_two, q_z, q_out, q_b, q_a, q_d1, q_d2, q_dz, q_d3, q_d4,
):
    rep, inner = lax.axis_index("rep"), lax.axis_index("inner")
    y, zl = lax.rem(rep, Y), rep // Y
    xc, zh = lax.rem(inner, XC), inner // XC
    up, down, far = lax.rem(y + 1, Y), lax.rem(y + 3, Y), lax.rem(y + 2, Y)
    right, left, pair = (zl * Y + up, inner), (zl * Y + down, inner), ((1 - zl) * Y + y, inner)

    def copy(src, dst, send, recv, to):
        return pltpu.make_async_remote_copy(
            src_ref=src, dst_ref=dst, send_sem=send, recv_sem=recv, device_id=to, device_id_type=MESH
        )

    def arrived(dst, recv):
        copy(dst, dst, s_one.at[0], recv, right).wait_recv()

    def left_it(src, send):
        copy(src, src, send, q_one.at[0], right).wait_send()


    @pl.loop(0, HALF)
    def _(k):
        copy(wp.at[far, k], r1p.at[k], s_one.at[k], q_one.at[k], right).start()
        copy(wp.at[far, HALF + k], r1m.at[k], s_one.at[HALF + k], q_one.at[HALF + k], left).start()

    @pl.loop(1, XC)
    def _(k):
        q = lax.rem(xc + k, XC)
        copy(cp.at[q], d1.at[xc], s_d1.at[q], q_d1.at[xc], (rep, zh * XC + q)).start()

    @pl.loop(0, HALF)
    def _(k):
        copy(wp.at[up, HALF + k], r2p.at[HALF + k], s_two.at[k], q_two.at[k], right).start()
        copy(wp.at[down, k], r2m.at[k], s_two.at[HALF + k], q_two.at[HALF + k], left).start()

    @pl.loop(1, OWNERS)
    def _(k):
        i = lax.rem(inner + k, OWNERS)
        copy(bp.at[i], brec.at[inner], s_b.at[i], q_b.at[inner], (rep, i)).start()

    brec[inner] = bp[inner]

    @pl.loop(0, HALF)
    def _(k):
        arrived(r1p.at[k], q_one.at[k])
        sp[k] = r1p[k] + wp[up, k]
        copy(sp.at[k], r2p.at[k], s_rel.at[k], q_two.at[MATS + k], right).start()
        arrived(r1m.at[k], q_one.at[HALF + k])
        sm[k] = r1m[k] + wp[down, HALF + k]
        copy(sm.at[k], r2m.at[HALF + k], s_rel.at[HALF + k], q_two.at[MATS + HALF + k], left).start()

    e2[...] = cp[xc]

    @pl.loop(1, XC)
    def _(k):
        q = lax.rem(xc + k, XC)
        arrived(d1.at[q], q_d1.at[q])
        e2[...] += d1[q]

    @pl.loop(1, Y)
    def _(k):
        t = lax.rem(y + k, Y)
        copy(e2.at[t], d2.at[y], s_d2.at[t], q_d2.at[y], (zl * Y + t, inner)).start()

    @pl.loop(0, HALF)
    def _(k):
        arrived(r2m.at[k], q_two.at[HALF + k])
        arrived(r2p.at[k], q_two.at[MATS + k])
        ssum[k] = wp[y, k] + r2p[k] + r2m[k]
        copy(ssum.at[k, 1 - zl], rz.at[k], s_z.at[k], q_z.at[k], pair).start()
        h = HALF + k
        arrived(r2p.at[h], q_two.at[k])
        arrived(r2m.at[h], q_two.at[MATS + h])
        ssum[h] = wp[y, h] + r2p[h] + r2m[h]
        copy(ssum.at[h, 1 - zl], rz.at[h], s_z.at[h], q_z.at[h], pair).start()

    f2[...] = e2[y]

    @pl.loop(1, Y)
    def _(k):
        t = lax.rem(y + k, Y)
        arrived(d2.at[t], q_d2.at[t])
        f2[...] += d2[t]

    copy(f2.at[1 - zl], d3.at[ZHI], s_dz.at[0], q_dz.at[0], pair).start()

    @pl.loop(1, OWNERS)
    def _(k):
        i = lax.rem(inner + k, OWNERS)
        arrived(brec.at[i], q_b.at[i])

    def gather(k, half):
        m = half * HALF + k
        arrived(rz.at[m], q_z.at[m])
        mean = (ssum[m, zl] + rz[m]) * (1.0 / GROUPS)
        avg[m] = mean
        out[y, m, zl] = AVERAGE_PART * mean + brec[list_ref[m]]
        mine = out.at[y, m, zl]
        copy(mine, mine, s_own.at[0, m], q_out.at[y, m, zl], pair).start()
        copy(mine, mine, s_own.at[1, m], q_out.at[y, m, zl], right).start()
        copy(mine, mine, s_own.at[2, m], q_out.at[y, m, zl], left).start()

    @pl.loop(0, HALF)
    def _(k):
        gather(k, 0)
        gather(k, 1)

    @pl.loop(0, OWNERS)
    def _(k):
        i = lax.rem(inner + k, OWNERS)
        picked = jnp.int32(0)
        for m in range(MATS):
            picked = picked + jnp.where(list_ref[m] == i, jnp.int32(m), jnp.int32(0))
        asend[i] = avg[jnp.minimum(picked, MATS - 1)]

    arec[inner] = asend[inner]

    @pl.loop(1, OWNERS)
    def _(k):
        i = lax.rem(inner + k, OWNERS)
        copy(asend.at[i], arec.at[inner], s_a.at[i], q_a.at[inner], (rep, i)).start()

    arrived(d3.at[ZHI], q_dz.at[0])
    g2[...] = f2[zl] + d3[ZHI]

    @pl.loop(1, ZHI)
    def _(k):
        t = lax.rem(zh + k, ZHI)
        copy(g2, d3.at[zh], s_d3.at[t], q_d3.at[zh], (rep, t * XC + xc)).start()

    def forward(m):
        other = out.at[y, m, 1 - zl]
        arrived(other, q_out.at[y, m, 1 - zl])
        copy(other, other, s_fwd.at[0, m], q_out.at[y, m, 1 - zl], right).start()
        copy(other, other, s_fwd.at[1, m], q_out.at[y, m, 1 - zl], left).start()

    @pl.loop(0, HALF)
    def _(k):
        forward(k)
        forward(HALF + k)

    d4[xc] = g2[...]

    @pl.loop(1, ZHI)
    def _(k):
        t = lax.rem(zh + k, ZHI)
        arrived(d3.at[t], q_d3.at[t])
        d4[xc] += d3[t]

    @pl.loop(1, XC)
    def _(k):
        q = lax.rem(xc + k, XC)
        copy(d4.at[xc], d4.at[xc], s_d4.at[q], q_d4.at[xc], (rep, zh * XC + q)).start()

    def relay(k, z):
        a = out.at[down, k, z]
        arrived(a, q_out.at[down, k, z])
        copy(a, a, s_far.at[0, k, z], q_out.at[down, k, z], right).start()
        b = out.at[up, HALF + k, z]
        arrived(b, q_out.at[up, HALF + k, z])
        copy(b, b, s_far.at[1, k, z], q_out.at[up, HALF + k, z], left).start()

    @pl.loop(0, HALF)
    def _(k):
        relay(k, zl)

    @pl.loop(0, HALF)
    def _(k):
        relay(k, 1 - zl)

    @pl.loop(0, HALF)
    def _(k):
        for z in range(ZLO):
            arrived(out.at[down, HALF + k, z], q_out.at[down, HALF + k, z])
            arrived(out.at[up, k, z], q_out.at[up, k, z])
            arrived(out.at[far, k, z], q_out.at[far, k, z])
            arrived(out.at[far, HALF + k, z], q_out.at[far, HALF + k, z])

    @pl.loop(1, XC)
    def _(k):
        q = lax.rem(xc + k, XC)
        arrived(d4.at[q], q_d4.at[q])

    coef[...] = d4[...]

    @pl.loop(1, OWNERS)
    def _(k):
        i = lax.rem(inner + k, OWNERS)
        arrived(arec.at[i], q_a.at[i])

    @pl.loop(0, HALF)
    def _(k):
        left_it(r1p.at[k], s_one.at[k])
        left_it(r1p.at[k], s_one.at[HALF + k])
        left_it(r1p.at[k], s_two.at[k])
        left_it(r1p.at[k], s_two.at[HALF + k])
        left_it(r1p.at[k], s_rel.at[k])
        left_it(r1p.at[k], s_rel.at[HALF + k])
        for h in range(2):
            left_it(rz.at[k], s_z.at[h * HALF + k])
            for n in range(3):
                left_it(rz.at[k], s_own.at[n, h * HALF + k])
            for n in range(2):
                left_it(rz.at[k], s_fwd.at[n, h * HALF + k])
                left_it(rz.at[k], s_far.at[n, k, h])

    @pl.loop(1, OWNERS)
    def _(k):
        i = lax.rem(inner + k, OWNERS)
        left_it(bp.at[i], s_b.at[i])
        left_it(asend.at[i], s_a.at[i])

    @pl.loop(1, XC)
    def _(k):
        q = lax.rem(xc + k, XC)
        left_it(cp.at[q], s_d1.at[q])
        left_it(g2, s_d4.at[q])

    @pl.loop(1, Y)
    def _(k):
        left_it(e2.at[0], s_d2.at[lax.rem(y + k, Y)])
        left_it(g2, s_d3.at[lax.rem(zh + k, ZHI)])

    left_it(g2, s_dz.at[0])


def unpack_kernel(list_ref, p_ref, a_ref, g_ref, m_ref, c_ref, cm_ref, bt_ref, gd_ref,
                  w_ref, mo_ref, nd_ref, cn_ref):
    p = p_ref[:, 0].transpose(1, 0, 2, 3)
    cols = jnp.stack([p[..., SLAB * g : SLAB * (g + 1)] for g in range(FOLD)], axis=2)
    w_ref[0] = cols.reshape(D, SLAB).T

    @pl.when(pl.program_id(0) == 0)
    def _():
        inner = lax.axis_index("inner")
        owns = jnp.int32(0)
        for m in range(MATS):
            owns = owns + jnp.where(list_ref[m] == inner, jnp.int32(1), jnp.int32(0))
        for g in range(FOLD):
            s = slice(SUB * g, SUB * (g + 1))
            mean = jnp.concatenate(
                [a_ref[i][:, SLAB * g : SLAB * (g + 1)] for i in range(OWNERS)], axis=-1
            )
            moment = outer_momentum * m_ref[s] + (g_ref[s] - mean)
            mo_ref[s] = jnp.where(owns > 0, moment, 0.0)

    @pl.when(pl.program_id(0) == 1)
    def _():
        step = c_ref[...].reshape(RANK, LANES)[:, :WIDTH]
        new = outer_momentum * cm_ref[...] + step
        cn_ref[...] = new
        change = lax.dot_general(
            bt_ref[...], step + outer_momentum * new, (((0,), (0,)), ((), ())),
            precision=HIGHEST, preferred_element_type=F32,
        )
        nd_ref[...] = gd_ref[...] - outer_rate * change


def shape(*s):
    return jax.ShapeDtypeStruct(s, F32)


def whole(*s):
    return pl.BlockSpec(s, lambda m: (0,) * len(s))


def on_device(weights, current, moment, owner_list, local_down, global_down, basis, coef_momentum):
    block = (SUB, LANES)
    low = (RANK // XC, LANES)
    g, mo, bt = current[0].T, moment[0].T, basis.T
    vmem = pl.BlockSpec(memory_space=pltpu.VMEM)
    smem = pl.BlockSpec(memory_space=pltpu.SMEM)
    wp, bp, cp = pl.pallas_call(
        pack_kernel,
        grid=(MATS,),
        in_specs=[
            pl.BlockSpec((1, SLAB, D), lambda m: (m, 0, 0)),
            whole(WIDTH, D), whole(WIDTH, D), whole(RANK, WIDTH), whole(WIDTH, D), whole(WIDTH, WIDTH),
        ],
        out_specs=[
            pl.BlockSpec((Y, 1, ZLO) + block, lambda m: (0, m, 0, 0, 0)),
            whole(OWNERS, *block),
            whole(XC, Y, ZLO, *low),
        ],
        out_shape=[shape(Y, MATS, ZLO, *block), shape(OWNERS, *block), shape(XC, Y, ZLO, *low)],
    )(weights[0], g, mo, bt, local_down[0], global_down)

    def buf(*s):
        return pltpu.VMEM(s, F32)

    dma = pltpu.SemaphoreType.DMA
    out, arec, coef = pl.pallas_call(
        comm_kernel,
        in_specs=[smem, vmem, vmem, vmem],
        out_specs=[vmem, vmem, vmem],
        out_shape=[shape(Y, MATS, ZLO, *block), shape(OWNERS, *block), shape(XC, *low)],
        scratch_shapes=[
            buf(HALF, ZLO, *block), buf(HALF, ZLO, *block), buf(MATS, ZLO, *block), buf(MATS, ZLO, *block),
            buf(HALF, ZLO, *block), buf(HALF, ZLO, *block), buf(MATS, *block), buf(MATS, ZLO, *block),
            buf(MATS, *block), buf(OWNERS, *block), buf(OWNERS, *block),
            buf(XC, Y, ZLO, *low), buf(Y, ZLO, *low), buf(ZHI + 1, *low), buf(XC, *low),
            buf(Y, ZLO, *low), buf(ZLO, *low), buf(*low),
            dma((MATS,)), dma((MATS,)), dma((MATS,)), dma((MATS,)), dma((3, MATS)), dma((2, MATS)),
            dma((2, HALF, ZLO)), dma((OWNERS,)), dma((OWNERS,)), dma((XC,)), dma((Y,)), dma((1,)),
            dma((ZHI,)), dma((XC,)),
            dma((MATS,)), dma((2 * MATS,)), dma((MATS,)), dma((Y, MATS, ZLO)), dma((OWNERS,)), dma((OWNERS,)),
            dma((XC,)), dma((Y,)), dma((1,)), dma((ZHI,)), dma((XC,)),
        ],
        compiler_params=pltpu.CompilerParams(has_side_effects=True, vmem_limit_bytes=60 * 2**20),
    )(owner_list, wp, bp, cp)

    new, momentum, new_down, coef_new = pl.pallas_call(
        unpack_kernel,
        grid=(MATS,),
        in_specs=[
            smem,
            pl.BlockSpec((Y, 1, ZLO) + block, lambda m: (0, m, 0, 0, 0)),
            whole(OWNERS, *block), whole(WIDTH, D), whole(WIDTH, D), whole(XC, *low), whole(RANK, WIDTH),
            whole(RANK, WIDTH), whole(WIDTH, WIDTH),
        ],
        out_specs=[
            pl.BlockSpec((1, SLAB, D), lambda m: (m, 0, 0)),
            whole(WIDTH, D), whole(WIDTH, WIDTH), whole(RANK, WIDTH),
        ],
        out_shape=[shape(MATS, SLAB, D), shape(WIDTH, D), shape(WIDTH, WIDTH), shape(RANK, WIDTH)],
    )(owner_list, out, arec, g, mo, coef, coef_momentum, bt, global_down)
    return new, momentum.T[None], new_down, coef_new


def solution(mesh):
    in_specs = (
        P("rep", None, "inner", None),
        P("inner", None, "rep"),
        P("inner", None, "rep"),
        P(),
        P("rep", "inner", None),
        P("inner", "rep"),
        P("inner", None),
        P(None, "rep"),
    )
    out_specs = (P(None, "inner", None), P("inner", None, "rep"), P("inner", "rep"), P(None, "rep"))
    return jax.shard_map(
        on_device, mesh=mesh, in_specs=in_specs, out_specs=out_specs, check_vma=False
    )
```

```python
import jax
import jax.numpy as jnp
from jax import lax
from jax.experimental import pallas as pl
from jax.experimental.pallas import tpu as pltpu
from jax.sharding import PartitionSpec as P

MESH = pl.DeviceIdType.MESH
HIGHEST = lax.Precision.HIGHEST
F32 = jnp.float32

outer_momentum = 0.9
outer_rate = 0.7

D = 1600
MATS = 12
HALF = MATS // 2
GROUPS = 8
OWNERS = 32
WIDTH = D // GROUPS
SLAB = D // OWNERS
RANK = 64
FOLD = 5
SUB = WIDTH // FOLD
LANES = 256
Y, ZLO, ZHI, XC = 4, 2, 4, 8

AVERAGE_PART = outer_rate * (1.0 + outer_momentum)
CURRENT_PART = 1.0 - AVERAGE_PART
MOMENT_PART = -outer_rate * outer_momentum * outer_momentum


def fold_lanes(parts):
    pad = jnp.zeros(parts[0].shape[:-1] + (LANES - FOLD * SLAB,), F32)
    return jnp.concatenate(list(parts) + [pad], axis=-1)


def comm_kernel(
    list_ref, w_hbm, g_hbm, m_hbm, ld_hbm, gd_ref, bt_ref, cm_ref,
    new_hbm, mo_ref, nd_ref, cn_ref,
    w_in, g_in, m_in, ld_in, cols, new, wp, bp, cp, out, arec, h_in, h_out,
    r1p, r1m, r2p, r2m, sp, sm, rz, ssum, avg, brec, asend,
    d1, d2, d3, d4, e2, f2, g2,
    s_one, s_two, s_rel, s_z, s_own, s_fwd, s_far, s_b, s_a, s_d1, s_d2, s_dz, s_d3, s_d4,
    q_one, q_two, q_z, q_out, q_b, q_a, q_d1, q_d2, q_dz, q_d3, q_d4,
):
    rep, inner = lax.axis_index("rep"), lax.axis_index("inner")
    y, zl = lax.rem(rep, Y), rep // Y
    xc, zh = lax.rem(inner, XC), inner // XC
    up, down, far = lax.rem(y + 1, Y), lax.rem(y + 3, Y), lax.rem(y + 2, Y)
    right, left, pair = (zl * Y + up, inner), (zl * Y + down, inner), ((1 - zl) * Y + y, inner)

    def copy(src, dst, send, recv, to):
        return pltpu.make_async_remote_copy(
            src_ref=src, dst_ref=dst, send_sem=send, recv_sem=recv, device_id=to, device_id_type=MESH
        )

    def arrived(dst, recv):
        copy(dst, dst, s_one.at[0], recv, right).wait_recv()

    def left_it(src, send):
        copy(src, src, send, q_one.at[0], right).wait_send()


    def fetch(m):
        return pltpu.make_async_copy(w_hbm.at[m, :, 0], w_in.at[m], h_in.at[m])

    @pl.loop(0, HALF)
    def _(k):
        fetch(k).start()
        fetch(HALF + k).start()

    rest = [
        pltpu.make_async_copy(g_hbm, g_in, h_in.at[MATS]),
        pltpu.make_async_copy(m_hbm, m_in, h_in.at[MATS + 1]),
        pltpu.make_async_copy(ld_hbm, ld_in, h_in.at[MATS + 2]),
    ]
    for c in rest:
        c.start()

    barrier = pltpu.get_barrier_semaphore()

    @pl.loop(1, OWNERS)
    def _(k):
        pl.semaphore_signal(
            barrier, inc=1, device_id=(rep, lax.rem(inner + k, OWNERS)), device_id_type=MESH
        )

    for to in (right, left, (zl * Y + far, inner), pair):
        pl.semaphore_signal(barrier, inc=1, device_id=to, device_id_type=MESH)

    def pack(m):
        fetch(m).wait()
        cols_m = w_in[m].T.reshape(ZLO, Y, FOLD, SUB, SLAB)
        wp[:, m] = fold_lanes([cols_m[:, :, g] for g in range(FOLD)]).transpose(1, 0, 2, 3)

    def first(k):
        copy(wp.at[far, k], r1p.at[k], s_one.at[k], q_one.at[k], right).start()
        copy(wp.at[far, HALF + k], r1m.at[k], s_one.at[HALF + k], q_one.at[HALF + k], left).start()
        copy(wp.at[up, HALF + k], r2p.at[HALF + k], s_two.at[k], q_two.at[k], right).start()
        copy(wp.at[down, k], r2m.at[k], s_two.at[HALF + k], q_two.at[HALF + k], left).start()

    pack(0)
    pack(HALF)
    pl.semaphore_wait(barrier, OWNERS + 3)
    first(0)

    rest[0].wait()
    rest[1].wait()
    term = (CURRENT_PART * g_in[...] + MOMENT_PART * m_in[...]).reshape(FOLD, SUB, D)
    for i in range(OWNERS):
        bp[i] = fold_lanes([term[g][:, SLAB * i : SLAB * (i + 1)] for g in range(FOLD)])

    @pl.loop(1, OWNERS)
    def _(k):
        i = lax.rem(inner + k, OWNERS)
        copy(bp.at[i], brec.at[inner], s_b.at[i], q_b.at[inner], (rep, i)).start()

    brec[inner] = bp[inner]

    @pl.loop(1, HALF)
    def _(k):
        pack(k)
        pack(HALF + k)
        first(k)

    rest[2].wait()
    local = jnp.dot(bt_ref[...], ld_in[...], precision=HIGHEST, preferred_element_type=F32)
    own = jnp.dot(bt_ref[...], gd_ref[...], precision=HIGHEST, preferred_element_type=F32)
    pad = jnp.zeros((RANK, LANES - WIDTH), F32)
    for r in range(GROUPS):
        part = local[:, WIDTH * r : WIDTH * (r + 1)] * (-1.0 / GROUPS)
        part = part + jnp.where(rep == r, own, 0.0)
        cp[:, r % Y, r // Y] = jnp.concatenate([part, pad], axis=-1).reshape(XC, RANK // XC, LANES)

    @pl.loop(1, XC)
    def _(k):
        q = lax.rem(xc + k, XC)
        copy(cp.at[q], d1.at[xc], s_d1.at[q], q_d1.at[xc], (rep, zh * XC + q)).start()

    @pl.loop(0, HALF)
    def _(k):
        arrived(r1p.at[k], q_one.at[k])
        sp[k] = r1p[k] + wp[up, k]
        copy(sp.at[k], r2p.at[k], s_rel.at[k], q_two.at[MATS + k], right).start()
        arrived(r1m.at[k], q_one.at[HALF + k])
        sm[k] = r1m[k] + wp[down, HALF + k]
        copy(sm.at[k], r2m.at[HALF + k], s_rel.at[HALF + k], q_two.at[MATS + HALF + k], left).start()

    e2[...] = cp[xc]

    @pl.loop(1, XC)
    def _(k):
        q = lax.rem(xc + k, XC)
        arrived(d1.at[q], q_d1.at[q])
        e2[...] += d1[q]

    @pl.loop(1, Y)
    def _(k):
        t = lax.rem(y + k, Y)
        copy(e2.at[t], d2.at[y], s_d2.at[t], q_d2.at[y], (zl * Y + t, inner)).start()

    @pl.loop(0, HALF)
    def _(k):
        arrived(r2m.at[k], q_two.at[HALF + k])
        arrived(r2p.at[k], q_two.at[MATS + k])
        ssum[k] = wp[y, k] + r2p[k] + r2m[k]
        copy(ssum.at[k, 1 - zl], rz.at[k], s_z.at[k], q_z.at[k], pair).start()
        h = HALF + k
        arrived(r2p.at[h], q_two.at[k])
        arrived(r2m.at[h], q_two.at[MATS + h])
        ssum[h] = wp[y, h] + r2p[h] + r2m[h]
        copy(ssum.at[h, 1 - zl], rz.at[h], s_z.at[h], q_z.at[h], pair).start()

    f2[...] = e2[y]

    @pl.loop(1, Y)
    def _(k):
        t = lax.rem(y + k, Y)
        arrived(d2.at[t], q_d2.at[t])
        f2[...] += d2[t]

    copy(f2.at[1 - zl], d3.at[ZHI], s_dz.at[0], q_dz.at[0], pair).start()

    @pl.loop(1, OWNERS)
    def _(k):
        i = lax.rem(inner + k, OWNERS)
        arrived(brec.at[i], q_b.at[i])

    def gather(k, half):
        m = half * HALF + k
        arrived(rz.at[m], q_z.at[m])
        mean = (ssum[m, zl] + rz[m]) * (1.0 / GROUPS)
        avg[m] = mean
        out[y, m, zl] = AVERAGE_PART * mean + brec[list_ref[m]]
        mine = out.at[y, m, zl]
        copy(mine, mine, s_own.at[0, m], q_out.at[y, m, zl], pair).start()
        copy(mine, mine, s_own.at[1, m], q_out.at[y, m, zl], right).start()
        copy(mine, mine, s_own.at[2, m], q_out.at[y, m, zl], left).start()

    def place(t, m, z):
        p = out[t, m, z]
        first_col = pl.multiple_of(WIDTH * (z * Y + t), 8)
        cols[m, pl.ds(first_col, WIDTH), :] = jnp.concatenate(
            [p[:, SLAB * g : SLAB * (g + 1)] for g in range(FOLD)], axis=0
        )

    @pl.loop(0, HALF)
    def _(k):
        gather(k, 0)
        gather(k, 1)

    @pl.loop(0, OWNERS)
    def _(k):
        i = lax.rem(inner + k, OWNERS)
        picked = jnp.int32(0)
        for m in range(MATS):
            picked = picked + jnp.where(list_ref[m] == i, jnp.int32(m), jnp.int32(0))
        asend[i] = avg[jnp.minimum(picked, MATS - 1)]

    arec[inner] = asend[inner]

    @pl.loop(1, OWNERS)
    def _(k):
        i = lax.rem(inner + k, OWNERS)
        copy(asend.at[i], arec.at[inner], s_a.at[i], q_a.at[inner], (rep, i)).start()

    arrived(d3.at[ZHI], q_dz.at[0])
    g2[...] = f2[zl] + d3[ZHI]

    @pl.loop(1, ZHI)
    def _(k):
        t = lax.rem(zh + k, ZHI)
        copy(g2, d3.at[zh], s_d3.at[t], q_d3.at[zh], (rep, t * XC + xc)).start()

    def forward(m):
        other = out.at[y, m, 1 - zl]
        arrived(other, q_out.at[y, m, 1 - zl])
        copy(other, other, s_fwd.at[0, m], q_out.at[y, m, 1 - zl], right).start()
        copy(other, other, s_fwd.at[1, m], q_out.at[y, m, 1 - zl], left).start()

    @pl.loop(0, HALF)
    def _(k):
        forward(k)
        forward(HALF + k)

    d4[xc] = g2[...]

    @pl.loop(1, ZHI)
    def _(k):
        t = lax.rem(zh + k, ZHI)
        arrived(d3.at[t], q_d3.at[t])
        d4[xc] += d3[t]

    @pl.loop(1, XC)
    def _(k):
        q = lax.rem(xc + k, XC)
        copy(d4.at[xc], d4.at[xc], s_d4.at[q], q_d4.at[xc], (rep, zh * XC + q)).start()

    def relay(k, z):
        a = out.at[down, k, z]
        arrived(a, q_out.at[down, k, z])
        copy(a, a, s_far.at[0, k, z], q_out.at[down, k, z], right).start()
        b = out.at[up, HALF + k, z]
        arrived(b, q_out.at[up, HALF + k, z])
        copy(b, b, s_far.at[1, k, z], q_out.at[up, HALF + k, z], left).start()
        place(down, k, z)
        place(up, HALF + k, z)

    @pl.loop(0, HALF)
    def _(k):
        relay(k, zl)
        place(y, k, zl)
        place(y, HALF + k, zl)

    @pl.loop(0, HALF)
    def _(k):
        relay(k, 1 - zl)
        place(y, k, 1 - zl)
        place(y, HALF + k, 1 - zl)

    @pl.loop(1, XC)
    def _(k):
        q = lax.rem(xc + k, XC)
        arrived(d4.at[q], q_d4.at[q])

    step = d4[...].reshape(RANK, LANES)[:, :WIDTH]
    coef = outer_momentum * cm_ref[...] + step
    cn_ref[...] = coef
    change = lax.dot_general(
        bt_ref[...], step + outer_momentum * coef, (((0,), (0,)), ((), ())),
        precision=HIGHEST, preferred_element_type=F32,
    )
    nd_ref[...] = gd_ref[...] - outer_rate * change

    @pl.loop(0, HALF)
    def _(k):
        for z in range(ZLO):
            arrived(out.at[down, HALF + k, z], q_out.at[down, HALF + k, z])
            place(down, HALF + k, z)
            arrived(out.at[up, k, z], q_out.at[up, k, z])
            place(up, k, z)

    def finish(m):
        for z in range(ZLO):
            arrived(out.at[far, m, z], q_out.at[far, m, z])
            place(far, m, z)
        new[m] = cols[m].T
        pltpu.make_async_copy(new.at[m], new_hbm.at[m], h_out.at[m]).start()

    @pl.loop(0, HALF)
    def _(k):
        finish(k)
        finish(HALF + k)

    @pl.loop(1, OWNERS)
    def _(k):
        i = lax.rem(inner + k, OWNERS)
        arrived(arec.at[i], q_a.at[i])

    owns = jnp.int32(0)
    for m in range(MATS):
        owns = owns + jnp.where(list_ref[m] == inner, jnp.int32(1), jnp.int32(0))
    for g in range(FOLD):
        s = slice(SUB * g, SUB * (g + 1))
        mean = jnp.concatenate(
            [arec[i][:, SLAB * g : SLAB * (g + 1)] for i in range(OWNERS)], axis=-1
        )
        moment = outer_momentum * m_in[s] + (g_in[s] - mean)
        mo_ref[s] = jnp.where(owns > 0, moment, 0.0)

    @pl.loop(0, HALF)
    def _(k):
        left_it(r1p.at[k], s_one.at[k])
        left_it(r1p.at[k], s_one.at[HALF + k])
        left_it(r1p.at[k], s_two.at[k])
        left_it(r1p.at[k], s_two.at[HALF + k])
        left_it(r1p.at[k], s_rel.at[k])
        left_it(r1p.at[k], s_rel.at[HALF + k])
        for h in range(2):
            left_it(rz.at[k], s_z.at[h * HALF + k])
            for n in range(3):
                left_it(rz.at[k], s_own.at[n, h * HALF + k])
            for n in range(2):
                left_it(rz.at[k], s_fwd.at[n, h * HALF + k])
                left_it(rz.at[k], s_far.at[n, k, h])

    @pl.loop(1, OWNERS)
    def _(k):
        i = lax.rem(inner + k, OWNERS)
        left_it(bp.at[i], s_b.at[i])
        left_it(asend.at[i], s_a.at[i])

    @pl.loop(1, XC)
    def _(k):
        q = lax.rem(xc + k, XC)
        left_it(cp.at[q], s_d1.at[q])
        left_it(g2, s_d4.at[q])

    @pl.loop(1, Y)
    def _(k):
        left_it(e2.at[0], s_d2.at[lax.rem(y + k, Y)])
        left_it(g2, s_d3.at[lax.rem(zh + k, ZHI)])

    left_it(g2, s_dz.at[0])

    @pl.loop(0, MATS)
    def _(m):
        pltpu.make_async_copy(new.at[m], new_hbm.at[m], h_out.at[m]).wait()


def shape(*s):
    return jax.ShapeDtypeStruct(s, F32)


def on_device(weights, current, moment, owner_list, local_down, global_down, basis, coef_momentum):
    block = (SUB, LANES)
    low = (RANK // XC, LANES)
    vmem = pl.BlockSpec(memory_space=pltpu.VMEM)
    smem = pl.BlockSpec(memory_space=pltpu.SMEM)
    hbm = pl.BlockSpec(memory_space=pl.ANY)

    def buf(*s):
        return pltpu.VMEM(s, F32)

    dma = pltpu.SemaphoreType.DMA
    new, momentum, new_down, coef_new = pl.pallas_call(
        comm_kernel,
        in_specs=[smem, hbm, hbm, hbm, hbm, vmem, vmem, vmem],
        out_specs=[hbm, vmem, vmem, vmem],
        out_shape=[shape(MATS, SLAB, D), shape(WIDTH, D), shape(WIDTH, WIDTH), shape(RANK, WIDTH)],
        scratch_shapes=[
            buf(MATS, SLAB, D), buf(WIDTH, D), buf(WIDTH, D), buf(WIDTH, D), buf(MATS, D, SLAB), buf(MATS, SLAB, D),
            buf(Y, MATS, ZLO, *block), buf(OWNERS, *block), buf(XC, Y, ZLO, *low), buf(Y, MATS, ZLO, *block),
            buf(OWNERS, *block), dma((MATS + 3,)), dma((MATS,)),
            buf(HALF, ZLO, *block), buf(HALF, ZLO, *block), buf(MATS, ZLO, *block), buf(MATS, ZLO, *block),
            buf(HALF, ZLO, *block), buf(HALF, ZLO, *block), buf(MATS, *block), buf(MATS, ZLO, *block),
            buf(MATS, *block), buf(OWNERS, *block), buf(OWNERS, *block),
            buf(XC, Y, ZLO, *low), buf(Y, ZLO, *low), buf(ZHI + 1, *low), buf(XC, *low),
            buf(Y, ZLO, *low), buf(ZLO, *low), buf(*low),
            dma((MATS,)), dma((MATS,)), dma((MATS,)), dma((MATS,)), dma((3, MATS)), dma((2, MATS)),
            dma((2, HALF, ZLO)), dma((OWNERS,)), dma((OWNERS,)), dma((XC,)), dma((Y,)), dma((1,)),
            dma((ZHI,)), dma((XC,)),
            dma((MATS,)), dma((2 * MATS,)), dma((MATS,)), dma((Y, MATS, ZLO)), dma((OWNERS,)), dma((OWNERS,)),
            dma((XC,)), dma((Y,)), dma((1,)), dma((ZHI,)), dma((XC,)),
        ],
        compiler_params=pltpu.CompilerParams(
            collective_id=0, has_side_effects=True, vmem_limit_bytes=60 * 2**20
        ),
    )(
        owner_list, weights.reshape(MATS, SLAB, 1, D), current[0].T, moment[0].T, local_down[0],
        global_down, basis.T, coef_momentum,
    )
    return new, momentum.T[None], new_down, coef_new


def solution(mesh):
    in_specs = (
        P("rep", None, "inner", None),
        P("inner", None, "rep"),
        P("inner", None, "rep"),
        P(),
        P("rep", "inner", None),
        P("inner", "rep"),
        P("inner", None),
        P(None, "rep"),
    )
    out_specs = (P(None, "inner", None), P("inner", None, "rep"), P("inner", "rep"), P(None, "rep"))
    return jax.shard_map(
        on_device, mesh=mesh, in_specs=in_specs, out_specs=out_specs, check_vma=False
    )
```

```python
import jax
import jax.numpy as jnp
from jax import lax
from jax.experimental import pallas as pl
from jax.experimental.pallas import tpu as pltpu
from jax.sharding import PartitionSpec as P

MESH = pl.DeviceIdType.MESH
HIGHEST = lax.Precision.HIGHEST
F32 = jnp.float32

outer_momentum = 0.9
outer_rate = 0.7

D = 1600
MATS = 12
HALF = MATS // 2
GROUPS = 8
OWNERS = 32
WIDTH = D // GROUPS
SLAB = D // OWNERS
RANK = 64
FOLD = 5
SUB = WIDTH // FOLD
LANES = 256
Y, ZLO, ZHI, XC = 4, 2, 4, 8

AVERAGE_PART = outer_rate * (1.0 + outer_momentum)
CURRENT_PART = 1.0 - AVERAGE_PART
MOMENT_PART = -outer_rate * outer_momentum * outer_momentum


def fold_lanes(parts):
    pad = jnp.zeros(parts[0].shape[:-1] + (LANES - FOLD * SLAB,), F32)
    return jnp.concatenate(list(parts) + [pad], axis=-1)


def comm_kernel(
    list_ref, w_hbm, g_hbm, m_hbm, ld_hbm, gd_ref, bt_ref, cm_ref,
    new_hbm, mo_ref, nd_ref, cn_ref,
    w_in, g_in, m_in, ld_in, cols, new, wp, bp, cp, out, arec, h_in, h_out,
    r1p, r1m, r2p, r2m, sp, sm, rz, ssum, avg, brec, asend,
    d1, d2, d3, d4, e2, f2, g2,
    s_one, s_two, s_rel, s_z, s_own, s_fwd, s_far, s_b, s_a, s_d1, s_d2, s_dz, s_d3, s_d4,
    q_one, q_two, q_z, q_out, q_b, q_a, q_d1, q_d2, q_dz, q_d3, q_d4,
):
    rep, inner = lax.axis_index("rep"), lax.axis_index("inner")
    y, zl = lax.rem(rep, Y), rep // Y
    xc, zh = lax.rem(inner, XC), inner // XC
    up, down, far = lax.rem(y + 1, Y), lax.rem(y + 3, Y), lax.rem(y + 2, Y)
    right, left, pair = (zl * Y + up, inner), (zl * Y + down, inner), ((1 - zl) * Y + y, inner)

    def copy(src, dst, send, recv, to):
        return pltpu.make_async_remote_copy(
            src_ref=src, dst_ref=dst, send_sem=send, recv_sem=recv, device_id=to, device_id_type=MESH
        )

    def arrived(dst, recv):
        copy(dst, dst, s_one.at[0], recv, right).wait_recv()

    def left_it(src, send):
        copy(src, src, send, q_one.at[0], right).wait_send()


    def fetch(m):
        return pltpu.make_async_copy(w_hbm.at[m, :, 0], w_in.at[m], h_in.at[m])

    @pl.loop(0, HALF)
    def _(k):
        fetch(k).start()
        fetch(HALF + k).start()

    rest = [
        pltpu.make_async_copy(g_hbm, g_in, h_in.at[MATS]),
        pltpu.make_async_copy(m_hbm, m_in, h_in.at[MATS + 1]),
        pltpu.make_async_copy(ld_hbm, ld_in, h_in.at[MATS + 2]),
    ]
    for c in rest:
        c.start()

    barrier = pltpu.get_barrier_semaphore()

    @pl.loop(1, OWNERS)
    def _(k):
        pl.semaphore_signal(
            barrier, inc=1, device_id=(rep, lax.rem(inner + k, OWNERS)), device_id_type=MESH
        )

    for to in (right, left, (zl * Y + far, inner), pair):
        pl.semaphore_signal(barrier, inc=1, device_id=to, device_id_type=MESH)

    def pack(m):
        fetch(m).wait()
        cols_m = w_in[m].T.reshape(ZLO, Y, FOLD, SUB, SLAB)
        wp[:, m] = fold_lanes([cols_m[:, :, g] for g in range(FOLD)]).transpose(1, 0, 2, 3)

    def first(k):
        copy(wp.at[far, k], r1p.at[k], s_one.at[k], q_one.at[k], right).start()
        copy(wp.at[far, HALF + k], r1m.at[k], s_one.at[HALF + k], q_one.at[HALF + k], left).start()
        copy(wp.at[up, HALF + k], r2p.at[HALF + k], s_two.at[k], q_two.at[k], right).start()
        copy(wp.at[down, k], r2m.at[k], s_two.at[HALF + k], q_two.at[HALF + k], left).start()

    pack(0)
    pack(HALF)
    rest[0].wait()
    rest[1].wait()
    term = (CURRENT_PART * g_in[...] + MOMENT_PART * m_in[...]).reshape(FOLD, SUB, D)
    for i in range(OWNERS):
        bp[i] = fold_lanes([term[g][:, SLAB * i : SLAB * (i + 1)] for g in range(FOLD)])

    pl.semaphore_wait(barrier, OWNERS + 3)
    first(0)

    def to_owners(send):
        @pl.loop(0, XC)
        def _(k):
            for dz in (2, 1, 3):
                send(lax.rem(zh + dz, ZHI) * XC + lax.rem(xc + k, XC))

        @pl.loop(1, XC)
        def _(k):
            send(zh * XC + lax.rem(xc + k, XC))

    def send_term(i):
        copy(bp.at[i], brec.at[inner], s_b.at[i], q_b.at[inner], (rep, i)).start()

    to_owners(send_term)
    brec[inner] = bp[inner]

    def second(k):
        arrived(r1p.at[k], q_one.at[k])
        sp[k] = r1p[k] + wp[up, k]
        copy(sp.at[k], r2p.at[k], s_rel.at[k], q_two.at[MATS + k], right).start()
        arrived(r1m.at[k], q_one.at[HALF + k])
        sm[k] = r1m[k] + wp[down, HALF + k]
        copy(sm.at[k], r2m.at[HALF + k], s_rel.at[HALF + k], q_two.at[MATS + HALF + k], left).start()

    pack(1)
    pack(HALF + 1)
    first(1)

    @pl.loop(2, HALF)
    def _(k):
        pack(k)
        pack(HALF + k)
        first(k)
        second(k - 2)

    rest[2].wait()
    local = jnp.dot(bt_ref[...], ld_in[...], precision=HIGHEST, preferred_element_type=F32)
    own = jnp.dot(bt_ref[...], gd_ref[...], precision=HIGHEST, preferred_element_type=F32)
    pad = jnp.zeros((RANK, LANES - WIDTH), F32)
    for r in range(GROUPS):
        part = local[:, WIDTH * r : WIDTH * (r + 1)] * (-1.0 / GROUPS)
        part = part + jnp.where(rep == r, own, 0.0)
        cp[:, r % Y, r // Y] = jnp.concatenate([part, pad], axis=-1).reshape(XC, RANK // XC, LANES)

    @pl.loop(1, XC)
    def _(k):
        q = lax.rem(xc + k, XC)
        copy(cp.at[q], d1.at[xc], s_d1.at[q], q_d1.at[xc], (rep, zh * XC + q)).start()

    @pl.loop(HALF - 2, HALF)
    def _(k):
        second(k)

    @pl.loop(0, HALF)
    def _(k):
        arrived(r2m.at[k], q_two.at[HALF + k])
        arrived(r2p.at[k], q_two.at[MATS + k])
        ssum[k] = wp[y, k] + r2p[k] + r2m[k]
        copy(ssum.at[k, 1 - zl], rz.at[k], s_z.at[k], q_z.at[k], pair).start()
        h = HALF + k
        arrived(r2p.at[h], q_two.at[k])
        arrived(r2m.at[h], q_two.at[MATS + h])
        ssum[h] = wp[y, h] + r2p[h] + r2m[h]
        copy(ssum.at[h, 1 - zl], rz.at[h], s_z.at[h], q_z.at[h], pair).start()

    e2[...] = cp[xc]

    @pl.loop(1, XC)
    def _(k):
        q = lax.rem(xc + k, XC)
        arrived(d1.at[q], q_d1.at[q])
        e2[...] += d1[q]

    @pl.loop(1, Y)
    def _(k):
        t = lax.rem(y + k, Y)
        copy(e2.at[t], d2.at[y], s_d2.at[t], q_d2.at[y], (zl * Y + t, inner)).start()

    @pl.loop(1, OWNERS)
    def _(k):
        i = lax.rem(inner + k, OWNERS)
        arrived(brec.at[i], q_b.at[i])

    def gather(k, half):
        m = half * HALF + k
        arrived(rz.at[m], q_z.at[m])
        mean = (ssum[m, zl] + rz[m]) * (1.0 / GROUPS)
        avg[m] = mean
        out[y, m, zl] = AVERAGE_PART * mean + brec[list_ref[m]]
        mine = out.at[y, m, zl]
        copy(mine, mine, s_own.at[0, m], q_out.at[y, m, zl], pair).start()
        copy(mine, mine, s_own.at[1, m], q_out.at[y, m, zl], right).start()
        copy(mine, mine, s_own.at[2, m], q_out.at[y, m, zl], left).start()

    def place(t, m, z):
        p = out[t, m, z]
        first_col = pl.multiple_of(WIDTH * (z * Y + t), 8)
        cols[m, pl.ds(first_col, WIDTH), :] = jnp.concatenate(
            [p[:, SLAB * g : SLAB * (g + 1)] for g in range(FOLD)], axis=0
        )

    @pl.loop(0, HALF)
    def _(k):
        gather(k, 0)
        gather(k, 1)

    def pick(i):
        picked = jnp.int32(0)
        for m in range(MATS):
            picked = picked + jnp.where(list_ref[m] == i, jnp.int32(m), jnp.int32(0))
        return avg[jnp.minimum(picked, MATS - 1)]

    def send_average(i):
        asend[i] = pick(i)
        copy(asend.at[i], arec.at[inner], s_a.at[i], q_a.at[inner], (rep, i)).start()

    to_owners(send_average)
    arec[inner] = pick(inner)

    f2[...] = e2[y]

    @pl.loop(1, Y)
    def _(k):
        t = lax.rem(y + k, Y)
        arrived(d2.at[t], q_d2.at[t])
        f2[...] += d2[t]

    copy(f2.at[1 - zl], d3.at[ZHI], s_dz.at[0], q_dz.at[0], pair).start()

    def forward(m):
        other = out.at[y, m, 1 - zl]
        arrived(other, q_out.at[y, m, 1 - zl])
        copy(other, other, s_fwd.at[0, m], q_out.at[y, m, 1 - zl], right).start()
        copy(other, other, s_fwd.at[1, m], q_out.at[y, m, 1 - zl], left).start()

    @pl.loop(0, HALF)
    def _(k):
        forward(k)
        forward(HALF + k)

    arrived(d3.at[ZHI], q_dz.at[0])
    g2[...] = f2[zl] + d3[ZHI]

    @pl.loop(1, ZHI)
    def _(k):
        t = lax.rem(zh + k, ZHI)
        copy(g2, d3.at[zh], s_d3.at[t], q_d3.at[zh], (rep, t * XC + xc)).start()

    def relay(k, z):
        a = out.at[down, k, z]
        arrived(a, q_out.at[down, k, z])
        copy(a, a, s_far.at[0, k, z], q_out.at[down, k, z], right).start()
        b = out.at[up, HALF + k, z]
        arrived(b, q_out.at[up, HALF + k, z])
        copy(b, b, s_far.at[1, k, z], q_out.at[up, HALF + k, z], left).start()
        place(down, k, z)
        place(up, HALF + k, z)

    @pl.loop(0, HALF)
    def _(k):
        relay(k, zl)
        place(y, k, zl)
        place(y, HALF + k, zl)

    d4[xc] = g2[...]

    @pl.loop(1, ZHI)
    def _(k):
        t = lax.rem(zh + k, ZHI)
        arrived(d3.at[t], q_d3.at[t])
        d4[xc] += d3[t]

    @pl.loop(1, XC)
    def _(k):
        q = lax.rem(xc + k, XC)
        copy(d4.at[xc], d4.at[xc], s_d4.at[q], q_d4.at[xc], (rep, zh * XC + q)).start()

    @pl.loop(0, HALF)
    def _(k):
        relay(k, 1 - zl)
        place(y, k, 1 - zl)
        place(y, HALF + k, 1 - zl)

    @pl.loop(1, XC)
    def _(k):
        q = lax.rem(xc + k, XC)
        arrived(d4.at[q], q_d4.at[q])

    step = d4[...].reshape(RANK, LANES)[:, :WIDTH]
    coef = outer_momentum * cm_ref[...] + step
    cn_ref[...] = coef
    change = lax.dot_general(
        bt_ref[...], step + outer_momentum * coef, (((0,), (0,)), ((), ())),
        precision=HIGHEST, preferred_element_type=F32,
    )
    nd_ref[...] = gd_ref[...] - outer_rate * change

    @pl.loop(0, HALF)
    def _(k):
        for z in range(ZLO):
            arrived(out.at[down, HALF + k, z], q_out.at[down, HALF + k, z])
            place(down, HALF + k, z)
            arrived(out.at[up, k, z], q_out.at[up, k, z])
            place(up, k, z)

    def finish(m):
        for z in range(ZLO):
            arrived(out.at[far, m, z], q_out.at[far, m, z])
            place(far, m, z)
        new[m] = cols[m].T
        pltpu.make_async_copy(new.at[m], new_hbm.at[m], h_out.at[m]).start()

    @pl.loop(0, HALF)
    def _(k):
        finish(k)
        finish(HALF + k)

    @pl.loop(1, OWNERS)
    def _(k):
        i = lax.rem(inner + k, OWNERS)
        arrived(arec.at[i], q_a.at[i])

    owns = jnp.int32(0)
    for m in range(MATS):
        owns = owns + jnp.where(list_ref[m] == inner, jnp.int32(1), jnp.int32(0))
    for g in range(FOLD):
        s = slice(SUB * g, SUB * (g + 1))
        mean = jnp.concatenate(
            [arec[i][:, SLAB * g : SLAB * (g + 1)] for i in range(OWNERS)], axis=-1
        )
        moment = outer_momentum * m_in[s] + (g_in[s] - mean)
        mo_ref[s] = jnp.where(owns > 0, moment, 0.0)

    @pl.loop(0, HALF)
    def _(k):
        left_it(r1p.at[k], s_one.at[k])
        left_it(r1p.at[k], s_one.at[HALF + k])
        left_it(r1p.at[k], s_two.at[k])
        left_it(r1p.at[k], s_two.at[HALF + k])
        left_it(r1p.at[k], s_rel.at[k])
        left_it(r1p.at[k], s_rel.at[HALF + k])
        for h in range(2):
            left_it(rz.at[k], s_z.at[h * HALF + k])
            for n in range(3):
                left_it(rz.at[k], s_own.at[n, h * HALF + k])
            for n in range(2):
                left_it(rz.at[k], s_fwd.at[n, h * HALF + k])
                left_it(rz.at[k], s_far.at[n, k, h])

    @pl.loop(1, OWNERS)
    def _(k):
        i = lax.rem(inner + k, OWNERS)
        left_it(bp.at[i], s_b.at[i])
        left_it(asend.at[i], s_a.at[i])

    @pl.loop(1, XC)
    def _(k):
        q = lax.rem(xc + k, XC)
        left_it(cp.at[q], s_d1.at[q])
        left_it(g2, s_d4.at[q])

    @pl.loop(1, Y)
    def _(k):
        left_it(e2.at[0], s_d2.at[lax.rem(y + k, Y)])
        left_it(g2, s_d3.at[lax.rem(zh + k, ZHI)])

    left_it(g2, s_dz.at[0])

    @pl.loop(0, MATS)
    def _(m):
        pltpu.make_async_copy(new.at[m], new_hbm.at[m], h_out.at[m]).wait()


def shape(*s):
    return jax.ShapeDtypeStruct(s, F32)


def on_device(weights, current, moment, owner_list, local_down, global_down, basis, coef_momentum):
    block = (SUB, LANES)
    low = (RANK // XC, LANES)
    vmem = pl.BlockSpec(memory_space=pltpu.VMEM)
    smem = pl.BlockSpec(memory_space=pltpu.SMEM)
    hbm = pl.BlockSpec(memory_space=pl.ANY)

    def buf(*s):
        return pltpu.VMEM(s, F32)

    dma = pltpu.SemaphoreType.DMA
    new, momentum, new_down, coef_new = pl.pallas_call(
        comm_kernel,
        in_specs=[smem, hbm, hbm, hbm, hbm, vmem, vmem, vmem],
        out_specs=[hbm, vmem, vmem, vmem],
        out_shape=[shape(MATS, SLAB, D), shape(WIDTH, D), shape(WIDTH, WIDTH), shape(RANK, WIDTH)],
        scratch_shapes=[
            buf(MATS, SLAB, D), buf(WIDTH, D), buf(WIDTH, D), buf(WIDTH, D), buf(MATS, D, SLAB), buf(MATS, SLAB, D),
            buf(Y, MATS, ZLO, *block), buf(OWNERS, *block), buf(XC, Y, ZLO, *low), buf(Y, MATS, ZLO, *block),
            buf(OWNERS, *block), dma((MATS + 3,)), dma((MATS,)),
            buf(HALF, ZLO, *block), buf(HALF, ZLO, *block), buf(MATS, ZLO, *block), buf(MATS, ZLO, *block),
            buf(HALF, ZLO, *block), buf(HALF, ZLO, *block), buf(MATS, *block), buf(MATS, ZLO, *block),
            buf(MATS, *block), buf(OWNERS, *block), buf(OWNERS, *block),
            buf(XC, Y, ZLO, *low), buf(Y, ZLO, *low), buf(ZHI + 1, *low), buf(XC, *low),
            buf(Y, ZLO, *low), buf(ZLO, *low), buf(*low),
            dma((MATS,)), dma((MATS,)), dma((MATS,)), dma((MATS,)), dma((3, MATS)), dma((2, MATS)),
            dma((2, HALF, ZLO)), dma((OWNERS,)), dma((OWNERS,)), dma((XC,)), dma((Y,)), dma((1,)),
            dma((ZHI,)), dma((XC,)),
            dma((MATS,)), dma((2 * MATS,)), dma((MATS,)), dma((Y, MATS, ZLO)), dma((OWNERS,)), dma((OWNERS,)),
            dma((XC,)), dma((Y,)), dma((1,)), dma((ZHI,)), dma((XC,)),
        ],
        compiler_params=pltpu.CompilerParams(
            collective_id=0, has_side_effects=True, vmem_limit_bytes=60 * 2**20
        ),
    )(
        owner_list, weights.reshape(MATS, SLAB, 1, D), current[0].T, moment[0].T, local_down[0],
        global_down, basis.T, coef_momentum,
    )
    return new, momentum.T[None], new_down, coef_new


def solution(mesh):
    in_specs = (
        P("rep", None, "inner", None),
        P("inner", None, "rep"),
        P("inner", None, "rep"),
        P(),
        P("rep", "inner", None),
        P("inner", "rep"),
        P("inner", None),
        P(None, "rep"),
    )
    out_specs = (P(None, "inner", None), P("inner", None, "rep"), P("inner", "rep"), P(None, "rep"))
    return jax.shard_map(
        on_device, mesh=mesh, in_specs=in_specs, out_specs=out_specs, check_vma=False
    )
```

```python
import jax
import jax.numpy as jnp
from jax import lax
from jax.experimental import pallas as pl
from jax.experimental.pallas import tpu as pltpu
from jax.sharding import PartitionSpec as P

MESH = pl.DeviceIdType.MESH
HIGHEST = lax.Precision.HIGHEST
F32 = jnp.float32

outer_momentum = 0.9
outer_rate = 0.7

D = 1600
MATS = 12
HALF = MATS // 2
GROUPS = 8
OWNERS = 32
WIDTH = D // GROUPS
SLAB = D // OWNERS
RANK = 64
FOLD = 5
SUB = WIDTH // FOLD
LANES = 256
Y, ZLO, ZHI, XC = 4, 2, 4, 8

AVERAGE_PART = outer_rate * (1.0 + outer_momentum)
CURRENT_PART = 1.0 - AVERAGE_PART
MOMENT_PART = -outer_rate * outer_momentum * outer_momentum


def fold_lanes(parts):
    pad = jnp.zeros(parts[0].shape[:-1] + (LANES - FOLD * SLAB,), F32)
    return jnp.concatenate(list(parts) + [pad], axis=-1)


def comm_kernel(
    list_ref, w_hbm, g_hbm, m_hbm, ld_hbm, gd_ref, bt_ref, cm_ref,
    new_hbm, mo_ref, nd_ref, cn_ref,
    w_in, g_in, m_in, ld_in, cols, new, wp, bp, cp, out, arec, h_in, h_out,
    r1p, r1m, r2p, r2m, sp, sm, rz, ssum, avg, brec, asend,
    d1, d2, d3, d4, e2, f2, g2,
    s_one, s_two, s_rel, s_z, s_own, s_fwd, s_far, s_b, s_a, s_d1, s_d2, s_dz, s_d3, s_d4,
    q_one, q_two, q_z, q_out, q_b, q_a, q_d1, q_d2, q_dz, q_d3, q_d4,
):
    rep, inner = lax.axis_index("rep"), lax.axis_index("inner")
    y, zl = lax.rem(rep, Y), rep // Y
    xc, zh = lax.rem(inner, XC), inner // XC
    up, down, far = lax.rem(y + 1, Y), lax.rem(y + 3, Y), lax.rem(y + 2, Y)
    right, left, pair = (zl * Y + up, inner), (zl * Y + down, inner), ((1 - zl) * Y + y, inner)

    def copy(src, dst, send, recv, to):
        return pltpu.make_async_remote_copy(
            src_ref=src, dst_ref=dst, send_sem=send, recv_sem=recv, device_id=to, device_id_type=MESH
        )

    def arrived(dst, recv):
        copy(dst, dst, s_one.at[0], recv, right).wait_recv()

    def left_it(src, send):
        copy(src, src, send, q_one.at[0], right).wait_send()


    def fetch(m):
        return pltpu.make_async_copy(w_hbm.at[m, :, 0], w_in.at[m], h_in.at[m])

    @pl.loop(0, HALF)
    def _(k):
        fetch(k).start()
        fetch(HALF + k).start()

    rest = [
        pltpu.make_async_copy(g_hbm, g_in, h_in.at[MATS]),
        pltpu.make_async_copy(m_hbm, m_in, h_in.at[MATS + 1]),
        pltpu.make_async_copy(ld_hbm, ld_in, h_in.at[MATS + 2]),
    ]
    for c in rest:
        c.start()

    barrier = pltpu.get_barrier_semaphore()

    @pl.loop(1, OWNERS)
    def _(k):
        pl.semaphore_signal(
            barrier, inc=1, device_id=(rep, lax.rem(inner + k, OWNERS)), device_id_type=MESH
        )

    for to in (right, left, (zl * Y + far, inner), pair):
        pl.semaphore_signal(barrier, inc=1, device_id=to, device_id_type=MESH)

    def pack(m):
        fetch(m).wait()
        cols_m = w_in[m].T.reshape(ZLO, Y, FOLD, SUB, SLAB)
        wp[:, m] = fold_lanes([cols_m[:, :, g] for g in range(FOLD)]).transpose(1, 0, 2, 3)

    def first(k):
        copy(wp.at[far, k], r1p.at[k], s_one.at[k], q_one.at[k], right).start()
        copy(wp.at[far, HALF + k], r1m.at[k], s_one.at[HALF + k], q_one.at[HALF + k], left).start()
        copy(wp.at[up, HALF + k], r2p.at[HALF + k], s_two.at[k], q_two.at[k], right).start()
        copy(wp.at[down, k], r2m.at[k], s_two.at[HALF + k], q_two.at[HALF + k], left).start()

    pack(0)
    pack(HALF)
    rest[0].wait()
    rest[1].wait()
    term = (CURRENT_PART * g_in[...] + MOMENT_PART * m_in[...]).reshape(FOLD, SUB, D)
    for i in range(OWNERS):
        bp[i] = fold_lanes([term[g][:, SLAB * i : SLAB * (i + 1)] for g in range(FOLD)])

    pl.semaphore_wait(barrier, OWNERS + 3)
    first(0)

    def to_owners(send):
        @pl.loop(0, XC)
        def _(k):
            for dz in (2, 1, 3):
                send(lax.rem(zh + dz, ZHI) * XC + lax.rem(xc + k, XC))

        @pl.loop(1, XC)
        def _(k):
            send(zh * XC + lax.rem(xc + k, XC))

    def send_term(i):
        copy(bp.at[i], brec.at[inner], s_b.at[i], q_b.at[inner], (rep, i)).start()

    to_owners(send_term)
    brec[inner] = bp[inner]

    def second(k):
        arrived(r1p.at[k], q_one.at[k])
        sp[k] = r1p[k] + wp[up, k]
        copy(sp.at[k], r2p.at[k], s_rel.at[k], q_two.at[MATS + k], right).start()
        arrived(r1m.at[k], q_one.at[HALF + k])
        sm[k] = r1m[k] + wp[down, HALF + k]
        copy(sm.at[k], r2m.at[HALF + k], s_rel.at[HALF + k], q_two.at[MATS + HALF + k], left).start()

    pack(1)
    pack(HALF + 1)
    first(1)

    @pl.loop(2, HALF)
    def _(k):
        pack(k)
        pack(HALF + k)
        first(k)
        second(k - 2)

    rest[2].wait()
    local = jnp.dot(bt_ref[...], ld_in[...], precision=HIGHEST, preferred_element_type=F32)
    own = jnp.dot(bt_ref[...], gd_ref[...], precision=HIGHEST, preferred_element_type=F32)
    pad = jnp.zeros((RANK, LANES - WIDTH), F32)
    for r in range(GROUPS):
        part = local[:, WIDTH * r : WIDTH * (r + 1)] * (-1.0 / GROUPS)
        part = part + jnp.where(rep == r, own, 0.0)
        cp[:, r % Y, r // Y] = jnp.concatenate([part, pad], axis=-1).reshape(XC, RANK // XC, LANES)

    @pl.loop(1, XC)
    def _(k):
        q = lax.rem(xc + k, XC)
        copy(cp.at[q], d1.at[xc], s_d1.at[q], q_d1.at[xc], (rep, zh * XC + q)).start()

    @pl.loop(HALF - 2, HALF)
    def _(k):
        second(k)

    @pl.loop(0, HALF)
    def _(k):
        arrived(r2m.at[k], q_two.at[HALF + k])
        arrived(r2p.at[k], q_two.at[MATS + k])
        ssum[k] = wp[y, k] + r2p[k] + r2m[k]
        copy(ssum.at[k, 1 - zl], rz.at[k], s_z.at[k], q_z.at[k], pair).start()
        h = HALF + k
        arrived(r2p.at[h], q_two.at[k])
        arrived(r2m.at[h], q_two.at[MATS + h])
        ssum[h] = wp[y, h] + r2p[h] + r2m[h]
        copy(ssum.at[h, 1 - zl], rz.at[h], s_z.at[h], q_z.at[h], pair).start()

    e2[...] = cp[xc]

    @pl.loop(1, XC)
    def _(k):
        q = lax.rem(xc + k, XC)
        arrived(d1.at[q], q_d1.at[q])
        e2[...] += d1[q]

    @pl.loop(1, Y)
    def _(k):
        t = lax.rem(y + k, Y)
        copy(e2.at[t], d2.at[y], s_d2.at[t], q_d2.at[y], (zl * Y + t, inner)).start()

    @pl.loop(1, OWNERS)
    def _(k):
        i = lax.rem(inner + k, OWNERS)
        arrived(brec.at[i], q_b.at[i])

    def gather(k, half):
        m = half * HALF + k
        arrived(rz.at[m], q_z.at[m])
        mean = (ssum[m, zl] + rz[m]) * (1.0 / GROUPS)
        avg[m] = mean
        out[y, m, zl] = AVERAGE_PART * mean + brec[list_ref[m]]
        mine = out.at[y, m, zl]
        copy(mine, mine, s_own.at[0, m], q_out.at[y, m, zl], pair).start()
        copy(mine, mine, s_own.at[1, m], q_out.at[y, m, zl], right).start()
        copy(mine, mine, s_own.at[2, m], q_out.at[y, m, zl], left).start()

    def place(t, m, z):
        p = out[t, m, z]
        first_col = pl.multiple_of(WIDTH * (z * Y + t), 8)
        cols[m, pl.ds(first_col, WIDTH), :] = jnp.concatenate(
            [p[:, SLAB * g : SLAB * (g + 1)] for g in range(FOLD)], axis=0
        )

    @pl.loop(0, HALF)
    def _(k):
        gather(k, 0)
        gather(k, 1)

    def pick(i):
        picked = jnp.int32(0)
        for m in range(MATS):
            picked = picked + jnp.where(list_ref[m] == i, jnp.int32(m), jnp.int32(0))
        return avg[jnp.minimum(picked, MATS - 1)]

    def send_average(i):
        asend[i] = pick(i)
        copy(asend.at[i], arec.at[inner], s_a.at[i], q_a.at[inner], (rep, i)).start()

    to_owners(send_average)
    arec[inner] = pick(inner)

    f2[...] = e2[y]

    @pl.loop(1, Y)
    def _(k):
        t = lax.rem(y + k, Y)
        arrived(d2.at[t], q_d2.at[t])
        f2[...] += d2[t]

    copy(f2.at[1 - zl], d3.at[ZHI], s_dz.at[0], q_dz.at[0], pair).start()

    def forward(m):
        other = out.at[y, m, 1 - zl]
        arrived(other, q_out.at[y, m, 1 - zl])
        copy(other, other, s_fwd.at[0, m], q_out.at[y, m, 1 - zl], right).start()
        copy(other, other, s_fwd.at[1, m], q_out.at[y, m, 1 - zl], left).start()

    @pl.loop(0, HALF)
    def _(k):
        forward(k)
        forward(HALF + k)

    arrived(d3.at[ZHI], q_dz.at[0])
    g2[...] = f2[zl] + d3[ZHI]

    @pl.loop(1, ZHI)
    def _(k):
        t = lax.rem(zh + k, ZHI)
        copy(g2, d3.at[zh], s_d3.at[t], q_d3.at[zh], (rep, t * XC + xc)).start()

    def relay(k, z):
        a = out.at[down, k, z]
        arrived(a, q_out.at[down, k, z])
        copy(a, a, s_far.at[0, k, z], q_out.at[down, k, z], right).start()
        b = out.at[up, HALF + k, z]
        arrived(b, q_out.at[up, HALF + k, z])
        copy(b, b, s_far.at[1, k, z], q_out.at[up, HALF + k, z], left).start()
        place(down, k, z)
        place(up, HALF + k, z)

    @pl.loop(0, HALF)
    def _(k):
        relay(k, zl)
        place(y, k, zl)
        place(y, HALF + k, zl)

    d4[xc] = g2[...]

    @pl.loop(1, ZHI)
    def _(k):
        t = lax.rem(zh + k, ZHI)
        arrived(d3.at[t], q_d3.at[t])
        d4[xc] += d3[t]

    @pl.loop(1, XC)
    def _(k):
        q = lax.rem(xc + k, XC)
        copy(d4.at[xc], d4.at[xc], s_d4.at[q], q_d4.at[xc], (rep, zh * XC + q)).start()

    def finish(m):
        for z in range(ZLO):
            arrived(out.at[far, m, z], q_out.at[far, m, z])
            place(far, m, z)
        new[m] = cols[m].T
        pltpu.make_async_copy(new.at[m], new_hbm.at[m], h_out.at[m]).start()

    def complete(k):
        for z in range(ZLO):
            arrived(out.at[down, HALF + k, z], q_out.at[down, HALF + k, z])
            place(down, HALF + k, z)
            arrived(out.at[up, k, z], q_out.at[up, k, z])
            place(up, k, z)
        finish(k)
        finish(HALF + k)

    def last_relay(k):
        relay(k, 1 - zl)
        place(y, k, 1 - zl)
        place(y, HALF + k, 1 - zl)

    @pl.loop(0, 2)
    def _(k):
        last_relay(k)

    @pl.loop(2, HALF)
    def _(k):
        last_relay(k)
        complete(k - 2)

    @pl.loop(1, XC)
    def _(k):
        q = lax.rem(xc + k, XC)
        arrived(d4.at[q], q_d4.at[q])

    step = d4[...].reshape(RANK, LANES)[:, :WIDTH]
    coef = outer_momentum * cm_ref[...] + step
    cn_ref[...] = coef
    change = lax.dot_general(
        bt_ref[...], step + outer_momentum * coef, (((0,), (0,)), ((), ())),
        precision=HIGHEST, preferred_element_type=F32,
    )
    nd_ref[...] = gd_ref[...] - outer_rate * change

    @pl.loop(HALF - 2, HALF)
    def _(k):
        complete(k)

    @pl.loop(1, OWNERS)
    def _(k):
        i = lax.rem(inner + k, OWNERS)
        arrived(arec.at[i], q_a.at[i])

    owns = jnp.int32(0)
    for m in range(MATS):
        owns = owns + jnp.where(list_ref[m] == inner, jnp.int32(1), jnp.int32(0))
    for g in range(FOLD):
        s = slice(SUB * g, SUB * (g + 1))
        mean = jnp.concatenate(
            [arec[i][:, SLAB * g : SLAB * (g + 1)] for i in range(OWNERS)], axis=-1
        )
        moment = outer_momentum * m_in[s] + (g_in[s] - mean)
        mo_ref[s] = jnp.where(owns > 0, moment, 0.0)

    @pl.loop(0, HALF)
    def _(k):
        left_it(r1p.at[k], s_one.at[k])
        left_it(r1p.at[k], s_one.at[HALF + k])
        left_it(r1p.at[k], s_two.at[k])
        left_it(r1p.at[k], s_two.at[HALF + k])
        left_it(r1p.at[k], s_rel.at[k])
        left_it(r1p.at[k], s_rel.at[HALF + k])
        for h in range(2):
            left_it(rz.at[k], s_z.at[h * HALF + k])
            for n in range(3):
                left_it(rz.at[k], s_own.at[n, h * HALF + k])
            for n in range(2):
                left_it(rz.at[k], s_fwd.at[n, h * HALF + k])
                left_it(rz.at[k], s_far.at[n, k, h])

    @pl.loop(1, OWNERS)
    def _(k):
        i = lax.rem(inner + k, OWNERS)
        left_it(bp.at[i], s_b.at[i])
        left_it(asend.at[i], s_a.at[i])

    @pl.loop(1, XC)
    def _(k):
        q = lax.rem(xc + k, XC)
        left_it(cp.at[q], s_d1.at[q])
        left_it(g2, s_d4.at[q])

    @pl.loop(1, Y)
    def _(k):
        left_it(e2.at[0], s_d2.at[lax.rem(y + k, Y)])
        left_it(g2, s_d3.at[lax.rem(zh + k, ZHI)])

    left_it(g2, s_dz.at[0])

    @pl.loop(0, MATS)
    def _(m):
        pltpu.make_async_copy(new.at[m], new_hbm.at[m], h_out.at[m]).wait()


def shape(*s):
    return jax.ShapeDtypeStruct(s, F32)


def on_device(weights, current, moment, owner_list, local_down, global_down, basis, coef_momentum):
    block = (SUB, LANES)
    low = (RANK // XC, LANES)
    vmem = pl.BlockSpec(memory_space=pltpu.VMEM)
    smem = pl.BlockSpec(memory_space=pltpu.SMEM)
    hbm = pl.BlockSpec(memory_space=pl.ANY)

    def buf(*s):
        return pltpu.VMEM(s, F32)

    dma = pltpu.SemaphoreType.DMA
    new, momentum, new_down, coef_new = pl.pallas_call(
        comm_kernel,
        in_specs=[smem, hbm, hbm, hbm, hbm, vmem, vmem, vmem],
        out_specs=[hbm, vmem, vmem, vmem],
        out_shape=[shape(MATS, SLAB, D), shape(WIDTH, D), shape(WIDTH, WIDTH), shape(RANK, WIDTH)],
        scratch_shapes=[
            buf(MATS, SLAB, D), buf(WIDTH, D), buf(WIDTH, D), buf(WIDTH, D), buf(MATS, D, SLAB), buf(MATS, SLAB, D),
            buf(Y, MATS, ZLO, *block), buf(OWNERS, *block), buf(XC, Y, ZLO, *low), buf(Y, MATS, ZLO, *block),
            buf(OWNERS, *block), dma((MATS + 3,)), dma((MATS,)),
            buf(HALF, ZLO, *block), buf(HALF, ZLO, *block), buf(MATS, ZLO, *block), buf(MATS, ZLO, *block),
            buf(HALF, ZLO, *block), buf(HALF, ZLO, *block), buf(MATS, *block), buf(MATS, ZLO, *block),
            buf(MATS, *block), buf(OWNERS, *block), buf(OWNERS, *block),
            buf(XC, Y, ZLO, *low), buf(Y, ZLO, *low), buf(ZHI + 1, *low), buf(XC, *low),
            buf(Y, ZLO, *low), buf(ZLO, *low), buf(*low),
            dma((MATS,)), dma((MATS,)), dma((MATS,)), dma((MATS,)), dma((3, MATS)), dma((2, MATS)),
            dma((2, HALF, ZLO)), dma((OWNERS,)), dma((OWNERS,)), dma((XC,)), dma((Y,)), dma((1,)),
            dma((ZHI,)), dma((XC,)),
            dma((MATS,)), dma((2 * MATS,)), dma((MATS,)), dma((Y, MATS, ZLO)), dma((OWNERS,)), dma((OWNERS,)),
            dma((XC,)), dma((Y,)), dma((1,)), dma((ZHI,)), dma((XC,)),
        ],
        compiler_params=pltpu.CompilerParams(
            collective_id=0, has_side_effects=True, vmem_limit_bytes=60 * 2**20
        ),
    )(
        owner_list, weights.reshape(MATS, SLAB, 1, D), current[0].T, moment[0].T, local_down[0],
        global_down, basis.T, coef_momentum,
    )
    return new, momentum.T[None], new_down, coef_new


def solution(mesh):
    in_specs = (
        P("rep", None, "inner", None),
        P("inner", None, "rep"),
        P("inner", None, "rep"),
        P(),
        P("rep", "inner", None),
        P("inner", "rep"),
        P("inner", None),
        P(None, "rep"),
    )
    out_specs = (P(None, "inner", None), P("inner", None, "rep"), P("inner", "rep"), P(None, "rep"))
    return jax.shard_map(
        on_device, mesh=mesh, in_specs=in_specs, out_specs=out_specs, check_vma=False
    )
```
